32 devices in a mesh: group: 2 (over y), scen: 16 (over z, x, core).
Axes of the slice: x: 2, y: 2, z: 4, core: 2. Of those that a mesh axis runs over, the one named last changes fastest.
Arguments:
- scenario_rows: bfloat16 [32, 2048, 2048], P(('group', 'scen')), parts along dimension 0, may hold values from -1 to 1
- barrier: float32 [32, 2048], P(('group', 'scen')), parts along dimension 0, may hold values from 0.01 to 61
- blocks: int32 [32, 6], P(('group', 'scen')), parts along dimension 0, may hold values from 0 to 15, all different within a row
- link_diag: float32 [4096], P('group'), parts along dimension 0, may hold values from 0.2 to 2
Outputs:
- factor: float32 [256, 16, 1024], P('group', 'scen'), parts along dimension 0
- trailing: float32 [128, 16, 1024], P('group', 'scen'), parts along dimension 0
The draws below stay inside these ranges and needn't reach their ends.
There are 2 independent parts, one for each index of `group`. The reference program is written for one: setup_inputs(seed, part) draws one part's arguments, and reference() takes and returns one part's arrays. A program takes and returns all parts, laid end to end along the dimension named above; each array names one. Nothing has to cross between parts.
Inputs may be any that keep to these rules, and one draw needn't show every extreme that they name: Each row names 6 distinct column blocks, and every block is named by some scenario.
All inputs are finite; a program needn't handle non-finite values.
Results may differ from the reference program's by a relative error of at most 0.0007.
Values sent between devices are 32-bit elements; how exact they have to be, the bound alone decides.
A program may use at most 128 MiB of HBM per device.

```python
import math
import jax
import jax.numpy as jnp
from jax import lax

K_DEV = 2048
BW = 128
NZB = 6
ROWS = 2048
SCENS = 16
N_SCEN = 16


def draw_barrier(key, part):
    common = jnp.exp(jax.random.uniform(jax.random.fold_in(key, 11), (K_DEV,), jnp.float32, math.log(0.03), math.log(30.0)))
    own = jnp.exp(jax.random.uniform(jax.random.fold_in(key, 12), (SCENS, K_DEV), jnp.float32, math.log(0.5), math.log(2.0)))
    return (common[None, :] * own).astype(jnp.float32)


def draw_scenario_rows(key, part):
    cover = SCENS * NZB * BW / ROWS
    unit = 1.0 / (cover * K_DEV * 4.7)
    common_scale = math.sqrt(unit)
    noise_scale = math.sqrt(0.5 * unit)
    base = jax.random.truncated_normal(jax.random.fold_in(key, 7), -4.0, 4.0, (K_DEV, ROWS), jnp.float32)
    noise = jax.random.truncated_normal(jax.random.fold_in(key, 8), -4.0, 4.0, (SCENS, K_DEV, ROWS), jnp.float32)
    values = common_scale * base[None, :, :] + noise_scale * noise
    return values.astype(jnp.bfloat16)


def distinct(own_key, rows, number_of, top, lift):
    ranking = jax.random.permutation(jax.random.fold_in(own_key, 1), number_of)
    boost = ranking
    for power in range(3):
        boost = boost * boost // number_of
    boost = boost * lift // number_of
    chance = jax.random.randint(jax.random.fold_in(own_key, 2), (rows, number_of), 0, 4096) + boost
    holders = jax.random.permutation(jax.random.fold_in(own_key, 3), rows)[jnp.arange(number_of) % rows]
    chance = jnp.where(jnp.arange(rows)[:, None] == holders[None, :], 1 << 14, chance)
    merit = chance * number_of + jnp.arange(number_of)
    return lax.top_k(merit.astype(jnp.int32), top)[1].astype(jnp.int32)


def setup_inputs(seed: int = 0, part: int = 0) -> dict:
    keys = jax.random.split(jax.random.key(seed), 5)
    part_keys = jax.random.split(jax.random.fold_in(keys[4], part), 5)
    scenario_rows = draw_scenario_rows(jax.random.fold_in(jax.random.fold_in(keys[4], part), 71), part)
    barrier = draw_barrier(jax.random.fold_in(jax.random.fold_in(keys[4], part), 71), part)
    blocks = distinct(part_keys[2], SCENS, ROWS // BW, NZB, 0)
    link_diag = jnp.clip(jnp.exp(jax.random.uniform(part_keys[3], (ROWS,), jnp.float32, math.log(0.2), math.log(2.0))), 0.2, 2.0)
    return {"scenario_rows": scenario_rows, "barrier": barrier, "blocks": blocks, "link_diag": link_diag}


def reference(scenario_rows, barrier, blocks, link_diag):
    rows_all = scenario_rows.shape[2]
    panel = rows_all // 2
    half = panel // 2
    column_block = jnp.arange(rows_all, dtype=jnp.int32) // BW

    def accumulate(carry, item):
        coupling, weights, listed = item
        keep = jnp.any(column_block[:, None] == listed[None, :], axis=1)
        masked = jnp.where(keep[None, :], coupling, jnp.zeros_like(coupling))
        weighted = (weights[:, None] * masked.astype(jnp.float32)).astype(jnp.bfloat16)
        left = weighted.astype(jnp.float32)
        right = masked.astype(jnp.float32)
        first = carry[0] + jnp.dot(left.T, right[:, :panel], precision=lax.Precision.HIGHEST)
        second = carry[1] + jnp.dot(left[:, panel:].T, right[:, panel:], precision=lax.Precision.HIGHEST)
        return ((first, second), None)
    start = (jnp.zeros((rows_all, panel), jnp.float32), jnp.zeros((panel, panel), jnp.float32))
    (first, second), unused = lax.scan(accumulate, start, (scenario_rows, barrier, blocks))
    first = first + jnp.concatenate([jnp.diag(link_diag[:panel]), jnp.zeros((panel, panel), jnp.float32)], axis=0)
    second = second + jnp.diag(link_diag[panel:])
    low_one = jnp.linalg.cholesky(first[:half, :half])
    rest_one = jax.scipy.linalg.solve_triangular(low_one, first[half:, :half].T, lower=True).T
    reduced = first[half:, half:] - jnp.dot(rest_one, rest_one[:half].T, precision=lax.Precision.HIGHEST)
    low_two = jnp.linalg.cholesky(reduced[:half])
    rest_two = jax.scipy.linalg.solve_triangular(low_two, reduced[half:].T, lower=True).T
    top = jnp.concatenate([low_one, jnp.zeros((half, half), jnp.float32)], axis=1)
    middle = jnp.concatenate([rest_one[:half], low_two], axis=1)
    bottom = jnp.concatenate([rest_one[half:], rest_two], axis=1)
    factor = jnp.concatenate([top, middle, bottom], axis=0)
    lower_rows = factor[panel:]
    trailing = second - jnp.dot(lower_rows, lower_rows.T, precision=lax.Precision.HIGHEST)
    return (factor.reshape(rows_all // N_SCEN, N_SCEN, panel), trailing.reshape(panel // N_SCEN, N_SCEN, panel))
```

```python
import functools

import jax
import jax.numpy as jnp
from jax import lax
from jax.experimental import pallas as pl
from jax.experimental.pallas import tpu as pltpu
from jax.sharding import PartitionSpec as P

BW = 128
HI = lax.Precision.HIGHEST


def contract(left, right, dims):
    return lax.dot_general(left, right, (dims, ((), ())), precision=HI, preferred_element_type=jnp.float32)


def gram_kernel(listed, *refs, touched, count):
    weights = refs[touched][...]
    out = refs[touched + 1]
    whole = refs[touched + 2]
    depth = weights.shape[1]
    right = jnp.concatenate([refs[i][...] for i in range(touched)], axis=1)
    for i in range(touched):
        turned = refs[i][...].T
        left = (weights * turned.astype(jnp.float32)).astype(jnp.bfloat16)
        part = lax.dot_general(left, right, (((1,), (0,)), ((), ())), preferred_element_type=jnp.float32)
        for j in range(touched):
            whole[j, i * BW : (i + 1) * BW, :] = part[:, j * BW : (j + 1) * BW]
    for owner in range(count):
        for j in range(touched):
            out[owner, :, j * BW : (j + 1) * BW] = whole[j, pl.ds(owner, touched * BW // count, stride=count), :]


def gram(coupling, weights, listed, count):
    depth, rows_all = coupling.shape
    touched = listed.shape[0]
    specs = [
        pl.BlockSpec((depth, BW), functools.partial(lambda i, step, names: (0, names[i]), i)) for i in range(touched)
    ]
    rows = touched * BW // count
    return pl.pallas_call(
        functools.partial(gram_kernel, touched=touched, count=count),
        out_shape=jax.ShapeDtypeStruct((count, rows, touched * BW), jnp.float32),
        grid_spec=pltpu.PrefetchScalarGridSpec(
            num_scalar_prefetch=1,
            grid=(1,),
            in_specs=specs + [pl.BlockSpec((1, depth), lambda step, names: (0, 0))],
            out_specs=pl.BlockSpec((count, rows, touched * BW), lambda step, names: (0, 0, 0)),
            scratch_shapes=[pltpu.VMEM((touched, touched * BW, BW), jnp.float32)],
        ),
        compiler_params=pltpu.CompilerParams(vmem_limit_bytes=50 * 1024 * 1024),
        name="gram",
    )(listed, *([coupling] * touched), weights)


def sum_kernel(listed, device, pieces, diag, out, *, touched, count):
    groups, each, columns = out.shape
    block = lax.broadcasted_iota(jnp.int32, out.shape, 0)
    inner = lax.broadcasted_iota(jnp.int32, out.shape, 1)
    column = lax.broadcasted_iota(jnp.int32, out.shape, 2)
    row = (block * each + inner) * count + device[0]
    out[...] = jnp.where(column == row, diag[...][None], 0.0)

    def add(source, carry):
        names = [listed[source * touched + i] for i in range(touched)]
        for i in range(touched):
            for j in range(touched):
                at = pl.ds(pl.multiple_of(names[j] * BW, BW), BW)
                out[names[i], :, at] += pieces[source, i * each : (i + 1) * each, j * BW : (j + 1) * BW]
        return carry

    lax.fori_loop(0, count, add, 0)


def sum_pieces(pieces, listed, device, diag, count):
    touched = listed.shape[1]
    each = BW // count
    rows_all = diag.shape[0]
    return pl.pallas_call(
        functools.partial(sum_kernel, touched=touched, count=count),
        out_shape=jax.ShapeDtypeStruct((rows_all // BW, each, rows_all), jnp.float32),
        in_specs=[
            pl.BlockSpec(memory_space=pltpu.SMEM),
            pl.BlockSpec(memory_space=pltpu.SMEM),
            pl.BlockSpec(memory_space=pltpu.VMEM),
            pl.BlockSpec(memory_space=pltpu.VMEM),
        ],
        out_specs=pl.BlockSpec(memory_space=pltpu.VMEM),
        compiler_params=pltpu.CompilerParams(vmem_limit_bytes=50 * 1024 * 1024),
        name="sum_pieces",
    )(listed.reshape(-1), device.reshape(1), pieces, diag[None, :])


def eliminate(tile):
    tiles = BW // 8
    sub = lax.broadcasted_iota(jnp.int32, (8, BW), 0)
    lane = lax.broadcasted_iota(jnp.int32, (8, BW), 1)
    a = [tile[8 * g : 8 * g + 8, :] for g in range(tiles)]
    v = [jnp.where(lane == sub + 8 * g, 1.0, 0.0).astype(jnp.float32) for g in range(tiles)]
    for j in range(0, BW, 2):
        g0, s0 = j // 8, j % 8
        row0, row1 = a[g0][s0 : s0 + 1, :], a[g0][s0 + 1 : s0 + 2, :]
        inv0, inv1 = v[g0][s0 : s0 + 1, :], v[g0][s0 + 1 : s0 + 2, :]
        pivot = row0[:, j : j + 1]
        cross = row0[:, j + 1 : j + 2]
        other = row1[:, j + 1 : j + 2]
        recip = 1.0 / pivot
        ratio = cross * recip
        recip1 = 1.0 / (other - cross * ratio)
        next_row = row1 - ratio * row0
        next_inv = inv1 - ratio * inv0
        row0s, inv0s = row0 * recip, inv0 * recip
        row1s, inv1s = next_row * recip1, next_inv * recip1
        for g in range(g0, tiles):
            c0 = jnp.broadcast_to(a[g][:, j : j + 1], (8, BW))
            c1 = jnp.broadcast_to(a[g][:, j + 1 : j + 2], (8, BW)) - c0 * ratio
            if g == g0:
                c0 = jnp.where(sub > s0, c0, 0.0)
                c1 = jnp.where(sub > s0 + 1, c1, 0.0)
            a[g] = a[g] - c0 * row0s - c1 * row1s
            v[g] = v[g] - c0 * inv0s - c1 * inv1s
    upper, inverse = [], []
    for g in range(tiles):
        own = jnp.sum(jnp.where(lane == sub + 8 * g, a[g], 0.0), axis=1, keepdims=True)
        scale = 1.0 / jnp.sqrt(own)
        upper.append(jnp.where(lane >= sub + 8 * g, a[g] * scale, 0.0))
        inverse.append(jnp.where(lane <= sub + 8 * g, v[g] * scale, 0.0))
    return jnp.concatenate(upper, axis=0).T, jnp.concatenate(inverse, axis=0)


def factor_kernel(top, own, low, rest, solved, work, inverses):
    half = top.shape[1]
    panel = 2 * half
    steps = panel // BW
    tail = own.shape[0]
    total = panel + tail
    for at in (0, half):
        square = top[2 * at : 2 * at + half, :]
        work[at : at + half, at : at + half] = 0.5 * (square + square.T)
    work[half:panel, :half] = top[half:panel, :]
    work[:half, half:] = jnp.zeros((half, half), jnp.float32)
    work[panel:, :] = own[...]
    low[...] = jnp.zeros_like(low)

    def step(b, carry):
        place = pl.ds(pl.multiple_of(b * BW, BW), BW)
        lower, inverse = eliminate(work[place, place])
        low[place, place] = lower
        inverses[b] = inverse
        for k in range(steps):

            @pl.when(b == k)
            def _():
                lo, hi = k * BW, (k + 1) * BW
                strip = contract(work[hi:total, lo:hi], inverses[k], ((1,), (1,)))
                rest[:, lo:hi] = strip[panel - hi :]
                if hi < panel:
                    low[hi:panel, lo:hi] = strip[: panel - hi]
                    for left in range(hi, panel, BW * 2):
                        right = min(left + BW * 2, panel)
                        work[left:total, left:right] -= contract(
                            strip[left - hi :], strip[left - hi : right - hi], ((1,), (1,))
                        )

        return carry

    lax.fori_loop(0, steps, step, 0)
    for k in range(steps - 1, -1, -1):
        lo, hi = k * BW, (k + 1) * BW
        value = rest[:, lo:hi]
        if hi < panel:
            value = value - contract(solved[:, hi:panel], low[hi:panel, lo:hi], ((1,), (0,)))
        solved[:, lo:hi] = contract(value, inverses[k], ((1,), (0,)))


def factorize(top, own):
    half = top.shape[1]
    panel = 2 * half
    tail = own.shape[0]
    return pl.pallas_call(
        factor_kernel,
        out_shape=(
            jax.ShapeDtypeStruct((panel, panel), jnp.float32),
            jax.ShapeDtypeStruct((tail, panel), jnp.float32),
            jax.ShapeDtypeStruct((tail, panel), jnp.float32),
        ),
        in_specs=[pl.BlockSpec(memory_space=pltpu.VMEM)] * 2,
        out_specs=(pl.BlockSpec(memory_space=pltpu.VMEM),) * 3,
        scratch_shapes=[
            pltpu.VMEM((panel + tail, panel), jnp.float32),
            pltpu.VMEM((panel // BW, BW, BW), jnp.float32),
        ],
        compiler_params=pltpu.CompilerParams(vmem_limit_bytes=50 * 1024 * 1024),
        cost_estimate=pl.CostEstimate(flops=80_000_000_000, bytes_accessed=12_000_000, transcendentals=0),
        name="factorize",
    )(top, own)


def shards(scenario_rows, barrier, blocks, link_diag):
    coupling = scenario_rows[0]
    listed = blocks[0]
    count = lax.axis_size("scen")
    device = lax.axis_index("scen").astype(jnp.int32)
    depth, rows_all = coupling.shape
    panel = rows_all // 2
    half = panel // 2
    own_rows = rows_all // count
    first_rows = half // count
    all_listed = lax.all_gather(listed, "scen")
    pieces = gram(coupling, barrier, listed, count)
    pieces = lax.all_to_all(pieces, "scen", 0, 0)
    sums = sum_pieces(pieces, all_listed, device, link_diag, count).reshape(own_rows, rows_all)
    head = jnp.concatenate([sums[: 2 * first_rows, :half], sums[first_rows : 2 * first_rows, half:panel]], axis=0)
    tail = sums[2 * first_rows :, :panel]
    top = lax.all_gather(head[:, None, :], "scen", axis=1, tiled=True)
    tail, top = lax.optimization_barrier((tail, top))
    bottom = lax.all_gather(tail[:, None, :], "scen", axis=1, tiled=True)
    low, rest, solved = factorize(top.reshape(3 * half, half), tail)
    own_low = lax.dynamic_index_in_dim(low.reshape(2 * first_rows, count, panel), device, 1, keepdims=False)
    factor = jnp.concatenate([own_low, rest], axis=0)
    second = sums[2 * first_rows :, panel:]
    update = jnp.einsum("rk,ink->rin", solved, bottom, precision=HI)
    trailing = second - update.reshape(second.shape)
    return (factor[:, None, :], trailing[:, None, :])


def solution(mesh):
    return jax.shard_map(
        shards,
        mesh=mesh,
        in_specs=(
            P(("group", "scen"), None, None),
            P(("group", "scen"), None),
            P(("group", "scen"), None),
            P("group"),
        ),
        out_specs=(P("group", "scen", None), P("group", "scen", None)),
        check_vma=False,
    )
```

```python
import functools

import jax
import jax.numpy as jnp
from jax import lax
from jax.experimental import pallas as pl
from jax.experimental.pallas import tpu as pltpu
from jax.sharding import PartitionSpec as P

BW = 128
WIDTH = 8
HI = lax.Precision.HIGHEST


def contract(left, right, dims):
    return lax.dot_general(left, right, (dims, ((), ())), precision=HI, preferred_element_type=jnp.float32)


def gram_kernel(listed, *refs, touched, count):
    weights = refs[touched][...]
    out = refs[touched + 1]
    whole = refs[touched + 2]
    depth = weights.shape[1]
    right = jnp.concatenate([refs[i][...] for i in range(touched)], axis=1)
    for i in range(touched):
        turned = refs[i][...].T
        left = (weights * turned.astype(jnp.float32)).astype(jnp.bfloat16)
        part = lax.dot_general(left, right, (((1,), (0,)), ((), ())), preferred_element_type=jnp.float32)
        for j in range(touched):
            whole[j, i * BW : (i + 1) * BW, :] = part[:, j * BW : (j + 1) * BW]
    for owner in range(count):
        for j in range(touched):
            out[owner, :, j * BW : (j + 1) * BW] = whole[j, pl.ds(owner, touched * BW // count, stride=count), :]


def gram(coupling, weights, listed, count):
    depth, rows_all = coupling.shape
    touched = listed.shape[0]
    specs = [
        pl.BlockSpec((depth, BW), functools.partial(lambda i, step, names: (0, names[i]), i)) for i in range(touched)
    ]
    rows = touched * BW // count
    return pl.pallas_call(
        functools.partial(gram_kernel, touched=touched, count=count),
        out_shape=jax.ShapeDtypeStruct((count, rows, touched * BW), jnp.float32),
        grid_spec=pltpu.PrefetchScalarGridSpec(
            num_scalar_prefetch=1,
            grid=(1,),
            in_specs=specs + [pl.BlockSpec((1, depth), lambda step, names: (0, 0))],
            out_specs=pl.BlockSpec((count, rows, touched * BW), lambda step, names: (0, 0, 0)),
            scratch_shapes=[pltpu.VMEM((touched, touched * BW, BW), jnp.float32)],
        ),
        compiler_params=pltpu.CompilerParams(vmem_limit_bytes=50 * 1024 * 1024),
        name="gram",
    )(listed, *([coupling] * touched), weights)


def sum_kernel(listed, device, pieces, diag, out, *, touched, count):
    groups, each, columns = out.shape
    block = lax.broadcasted_iota(jnp.int32, out.shape, 0)
    inner = lax.broadcasted_iota(jnp.int32, out.shape, 1)
    column = lax.broadcasted_iota(jnp.int32, out.shape, 2)
    row = (block * each + inner) * count + device[0]
    out[...] = jnp.where(column == row, diag[...][None], 0.0)

    def add(source, carry):
        names = [listed[source * touched + i] for i in range(touched)]
        for i in range(touched):
            for j in range(touched):
                at = pl.ds(pl.multiple_of(names[j] * BW, BW), BW)
                out[names[i], :, at] += pieces[source, i * each : (i + 1) * each, j * BW : (j + 1) * BW]
        return carry

    lax.fori_loop(0, count, add, 0)


def sum_pieces(pieces, listed, device, diag, count):
    touched = listed.shape[1]
    each = BW // count
    rows_all = diag.shape[0]
    return pl.pallas_call(
        functools.partial(sum_kernel, touched=touched, count=count),
        out_shape=jax.ShapeDtypeStruct((rows_all // BW, each, rows_all), jnp.float32),
        in_specs=[
            pl.BlockSpec(memory_space=pltpu.SMEM),
            pl.BlockSpec(memory_space=pltpu.SMEM),
            pl.BlockSpec(memory_space=pltpu.VMEM),
            pl.BlockSpec(memory_space=pltpu.VMEM),
        ],
        out_specs=pl.BlockSpec(memory_space=pltpu.VMEM),
        compiler_params=pltpu.CompilerParams(vmem_limit_bytes=50 * 1024 * 1024),
        name="sum_pieces",
    )(listed.reshape(-1), device.reshape(1), pieces, diag[None, :])


def eliminate(tile, width=WIDTH):
    tiles = BW // 8
    sub = lax.broadcasted_iota(jnp.int32, (8, BW), 0)
    lane = lax.broadcasted_iota(jnp.int32, (8, BW), 1)
    a = [tile[8 * g : 8 * g + 8, :] for g in range(tiles)]
    v = [jnp.where(lane == sub + 8 * g, 1.0, 0.0).astype(jnp.float32) for g in range(tiles)]
    for j in range(0, BW, width):
        g0, s0 = j // 8, j % 8
        rows = [jnp.broadcast_to(a[g0][s0 + t : s0 + t + 1, :], (8, BW)) for t in range(width)]
        invs = [jnp.broadcast_to(v[g0][s0 + t : s0 + t + 1, :], (8, BW)) for t in range(width)]
        core = [
            [jnp.broadcast_to(rows[t][:, j + u : j + u + 1], (8, BW)) for u in range(width)] for t in range(width)
        ]
        ratios = []
        for t in range(width):
            recip = 1.0 / core[t][t]
            ratio = [core[t][u] * recip for u in range(width)]
            for u in range(t + 1, width):
                for w in range(u, width):
                    core[u][w] = core[u][w] - ratio[u] * core[t][w]
                rows[u] = rows[u] - ratio[u] * rows[t]
                invs[u] = invs[u] - ratio[u] * invs[t]
            ratios.append(ratio)
            rows[t], invs[t] = rows[t] * recip, invs[t] * recip
        for g in range(g0, tiles):
            own = [jnp.broadcast_to(a[g][:, j + t : j + t + 1], (8, BW)) for t in range(width)]
            for t in range(width):
                for u in range(t + 1, width):
                    own[u] = own[u] - own[t] * ratios[t][u]
            for t in range(width):
                use = jnp.where(sub > s0 + t, own[t], 0.0) if g == g0 else own[t]
                a[g] = a[g] - use * rows[t]
                v[g] = v[g] - use * invs[t]
    upper, inverse = [], []
    for g in range(tiles):
        own = jnp.sum(jnp.where(lane == sub + 8 * g, a[g], 0.0), axis=1, keepdims=True)
        scale = 1.0 / jnp.sqrt(own)
        upper.append(jnp.where(lane >= sub + 8 * g, a[g] * scale, 0.0))
        inverse.append(jnp.where(lane <= sub + 8 * g, v[g] * scale, 0.0))
    return jnp.concatenate(upper, axis=0).T, jnp.concatenate(inverse, axis=0)


def factor_kernel(top, own, low, rest, solved, work, inverses):
    half = top.shape[1]
    panel = 2 * half
    steps = panel // BW
    tail = own.shape[0]
    total = panel + tail
    for at in (0, half):
        square = top[2 * at : 2 * at + half, :]
        work[at : at + half, at : at + half] = 0.5 * (square + square.T)
    work[half:panel, :half] = top[half:panel, :]
    work[:half, half:] = jnp.zeros((half, half), jnp.float32)
    work[panel:, :] = own[...]
    low[...] = jnp.zeros_like(low)

    def step(b, carry):
        place = pl.ds(pl.multiple_of(b * BW, BW), BW)
        lower, inverse = eliminate(work[place, place])
        low[place, place] = lower
        inverses[b] = inverse
        for k in range(steps):

            @pl.when(b == k)
            def _():
                lo, hi = k * BW, (k + 1) * BW
                strip = contract(work[hi:total, lo:hi], inverses[k], ((1,), (1,)))
                rest[:, lo:hi] = strip[panel - hi :]
                if hi < panel:
                    low[hi:panel, lo:hi] = strip[: panel - hi]
                    for left in range(hi, panel, BW * 2):
                        right = min(left + BW * 2, panel)
                        work[left:total, left:right] -= contract(
                            strip[left - hi :], strip[left - hi : right - hi], ((1,), (1,))
                        )

        return carry

    lax.fori_loop(0, steps, step, 0)
    for k in range(steps - 1, -1, -1):
        lo, hi = k * BW, (k + 1) * BW
        value = rest[:, lo:hi]
        if hi < panel:
            value = value - contract(solved[:, hi:panel], low[hi:panel, lo:hi], ((1,), (0,)))
        solved[:, lo:hi] = contract(value, inverses[k], ((1,), (0,)))


def factorize(top, own):
    half = top.shape[1]
    panel = 2 * half
    tail = own.shape[0]
    return pl.pallas_call(
        factor_kernel,
        out_shape=(
            jax.ShapeDtypeStruct((panel, panel), jnp.float32),
            jax.ShapeDtypeStruct((tail, panel), jnp.float32),
            jax.ShapeDtypeStruct((tail, panel), jnp.float32),
        ),
        in_specs=[pl.BlockSpec(memory_space=pltpu.VMEM)] * 2,
        out_specs=(pl.BlockSpec(memory_space=pltpu.VMEM),) * 3,
        scratch_shapes=[
            pltpu.VMEM((panel + tail, panel), jnp.float32),
            pltpu.VMEM((panel // BW, BW, BW), jnp.float32),
        ],
        compiler_params=pltpu.CompilerParams(vmem_limit_bytes=50 * 1024 * 1024),
        cost_estimate=pl.CostEstimate(flops=80_000_000_000, bytes_accessed=12_000_000, transcendentals=0),
        name="factorize",
    )(top, own)


def shards(scenario_rows, barrier, blocks, link_diag):
    coupling = scenario_rows[0]
    listed = blocks[0]
    count = lax.axis_size("scen")
    device = lax.axis_index("scen").astype(jnp.int32)
    depth, rows_all = coupling.shape
    panel = rows_all // 2
    half = panel // 2
    own_rows = rows_all // count
    first_rows = half // count
    all_listed = lax.all_gather(listed, "scen")
    pieces = gram(coupling, barrier, listed, count)
    pieces = lax.all_to_all(pieces, "scen", 0, 0)
    sums = sum_pieces(pieces, all_listed, device, link_diag, count).reshape(own_rows, rows_all)
    head = jnp.concatenate([sums[: 2 * first_rows, :half], sums[first_rows : 2 * first_rows, half:panel]], axis=0)
    tail = sums[2 * first_rows :, :panel]
    top = lax.all_gather(head[:, None, :], "scen", axis=1, tiled=True)
    tail, top = lax.optimization_barrier((tail, top))
    bottom = lax.all_gather(tail[:, None, :], "scen", axis=1, tiled=True)
    low, rest, solved = factorize(top.reshape(3 * half, half), tail)
    own_low = lax.dynamic_index_in_dim(low.reshape(2 * first_rows, count, panel), device, 1, keepdims=False)
    factor = jnp.concatenate([own_low, rest], axis=0)
    second = sums[2 * first_rows :, panel:]
    update = jnp.einsum("rk,ink->rin", solved, bottom, precision=HI)
    trailing = second - update.reshape(second.shape)
    return (factor[:, None, :], trailing[:, None, :])


def solution(mesh):
    return jax.shard_map(
        shards,
        mesh=mesh,
        in_specs=(
            P(("group", "scen"), None, None),
            P(("group", "scen"), None),
            P(("group", "scen"), None),
            P("group"),
        ),
        out_specs=(P("group", "scen", None), P("group", "scen", None)),
        check_vma=False,
    )
```
